32 devices in a mesh: dp: 32 (over z, y, x, core).
Axes of the slice: x: 2, y: 2, z: 4, core: 2. Of those that a mesh axis runs over, the one named last changes fastest.
Arguments:
- stream: float32 [4096, 960], P('dp'), may hold values from -6 to 6
- segments: int32 [4096], P('dp'), may hold values from -1 to 7, as said below
- cotangent: float32 [4096, 960], P('dp'), may hold values from -6 to 6
- attn_gain: float32 [960], replicated, may hold values from 0.25 to 1.75
- mlp_gain: float32 [960], replicated, may hold values from 0.25 to 1.75
- w_query: bfloat16 [921600], P('dp'), may hold values from -0.1875 to 0.1875
- w_key: bfloat16 [307200], P('dp'), may hold values from -0.1875 to 0.1875
- w_value: bfloat16 [307200], P('dp'), may hold values from -0.1875 to 0.1875
- w_out: bfloat16 [921600], P('dp'), may hold values from -0.75 to 0.75
- w_gate: bfloat16 [2457600], P('dp'), may hold values from -0.1875 to 0.1875
- w_up: bfloat16 [2457600], P('dp'), may hold values from -0.1875 to 0.1875
- w_down: bfloat16 [2457600], P('dp'), may hold values from -0.125 to 0.125
Outputs:
- output: float32 [4096, 960], P('dp')
- grad_x: float32 [4096, 960], P('dp')
- grad_query: float32 [921600], P('dp')
- grad_key: float32 [307200], P('dp')
- grad_value: float32 [307200], P('dp')
- grad_out: float32 [921600], P('dp')
- grad_gate: float32 [2457600], P('dp')
- grad_up: float32 [2457600], P('dp')
- grad_down: float32 [2457600], P('dp')
- grad_attn_gain: float32 [960], replicated
- grad_mlp_gain: float32 [960], replicated
The draws below stay inside these ranges and needn't reach their ends.
Inputs may be any that keep to these rules, and one draw needn't show every extreme that they name: `segments`: within each aligned block of 64 rows the used slots come first and carry segment numbers 0, 1, 2, ... in runs of consecutive rows, never falling; the remaining slots hold -1. The first block of every device is full.
All inputs are finite; a program needn't handle non-finite values.
Results may differ from the reference program's by a relative error of at most 0.012.
Values may be sent and summed in bfloat16 or wider, within the bound.
A program may use at most 256 MiB of HBM per device.

```python
import math
import jax
import jax.numpy as jnp
from jax import lax

D = 960
H = 15
KV = 5
HD = 64
FF = 2560
MB_ROWS = 64
MBATCH = 2
GROUP = 3
TOKENS = 4096


def draw_segments(key, part):
    blocks = TOKENS // MB_ROWS
    ceiling = MB_ROWS // 8 - 1
    first_key = jax.random.fold_in(key, 11)
    second_key = jax.random.fold_in(key, 23)
    live_count = jax.random.randint(first_key, (blocks,), MB_ROWS // 8, MB_ROWS + 1)
    block_index = jnp.arange(blocks)
    live_count = jnp.where(block_index % MBATCH == 0, MB_ROWS, live_count)
    live_count = jnp.where(block_index == blocks - 1, MB_ROWS // 2, live_count)
    starts = jax.random.randint(second_key, (blocks, MB_ROWS), 0, 24) == 0
    column = jnp.arange(MB_ROWS)
    starts = starts & (column[None, :] > 0)
    numbers = jnp.minimum(jnp.cumsum(starts.astype(jnp.int32), axis=1), ceiling)
    spread = column * (ceiling + 1) // MB_ROWS
    numbers = jnp.where((block_index % MBATCH == 0)[:, None], spread[None, :], numbers)
    numbers = jnp.where(column[None, :] < live_count[:, None], numbers, -1)
    return numbers.reshape(-1).astype(jnp.int32)


def shard_levels(key, extent, shards, smallest, high):
    loudness, own = 1.0, jax.random.fold_in(key, 6)
    for dim, blocks in shards:
        steps = jnp.exp(jax.random.uniform(jax.random.fold_in(own, dim), (blocks,), jnp.float32, smallest / len(shards), high / len(shards)))
        loudness = loudness * jnp.repeat(steps, extent[dim] // blocks).reshape([-1 if axis == dim else 1 for axis in range(len(extent))])
    return loudness


def gaussian(key, dims, width, limit, shards=(), kind=jnp.bfloat16):
    drawn = jax.random.normal(key, dims, jnp.float32) * width
    if len(shards) > 0:
        drawn = shard_levels(key, dims, shards, -0.22, 0.18) * drawn
    return jnp.clip(drawn, min=-limit, max=limit).astype(kind)


def setup_inputs(seed: int = 0) -> dict:
    seeds = jax.random.split(jax.random.key(seed), 13)
    stream = gaussian(seeds[0], (TOKENS, D), 1.0, 6.0, ((0, 32),), jnp.float32)
    segments = draw_segments(jax.random.fold_in(seeds[12], 71), 0)
    cotangent = gaussian(seeds[2], (TOKENS, D), 1.0, 6.0, ((0, 32),), jnp.float32)
    attn_gain = jnp.clip(1.0 + 0.15 * jax.random.normal(seeds[3], (D,), jnp.float32), 0.25, 1.75)
    mlp_gain = jnp.clip(1.0 + 0.15 * jax.random.normal(seeds[4], (D,), jnp.float32), 0.25, 1.75)
    w_query = gaussian(seeds[5], (D * D,), D ** -0.5, 0.1875, ((0, 32),))
    w_key = gaussian(seeds[6], (D * KV * HD,), D ** -0.5, 0.1875, ((0, 32),))
    w_value = gaussian(seeds[7], (D * KV * HD,), D ** -0.5, 0.1875, ((0, 32),))
    w_out = gaussian(seeds[8], (D * D,), (D // 16) ** -0.5, 0.75, ((0, 32),))
    w_gate = gaussian(seeds[9], (D * FF,), D ** -0.5, 0.1875, ((0, 32),))
    w_up = gaussian(seeds[10], (D * FF,), D ** -0.5, 0.1875, ((0, 32),))
    w_down = gaussian(seeds[11], (FF * D,), FF ** -0.5, 0.125, ((0, 32),))
    return {"stream": stream, "segments": segments, "cotangent": cotangent, "attn_gain": attn_gain, "mlp_gain": mlp_gain, "w_query": w_query, "w_key": w_key, "w_value": w_value, "w_out": w_out, "w_gate": w_gate, "w_up": w_up, "w_down": w_down}


EPSILON = 1e-05
ROPE_BASE = 10000.0

def inverse_root(values):
    return lax.rsqrt(lax.optimization_barrier(jnp.mean(values * values, axis=-1, keepdims=True)) + EPSILON)

def rotary_tables(block_segments):
    row_count = block_segments.shape[-1]
    row_index = jnp.arange(row_count)
    earlier = (block_segments[:, :, None] == block_segments[:, None, :]) & (row_index[None, None, :] < row_index[None, :, None])
    position = lax.optimization_barrier(jnp.sum(earlier.astype(jnp.float32), axis=-1))
    half_size = HD // 2
    frequency = ROPE_BASE ** (-2.0 * jnp.arange(half_size, dtype=jnp.float32) / HD)
    angle_table = position[:, :, None, None] * frequency
    return (jnp.cos(angle_table), jnp.sin(angle_table))

def allowed_pairs(block_segments):
    row_count = block_segments.shape[-1]
    row_index = jnp.arange(row_count)
    causal = row_index[None, :] <= row_index[:, None]
    diagonal = row_index[None, :] == row_index[:, None]
    same_segment = (block_segments[:, :, None] == block_segments[:, None, :]) & (block_segments[:, :, None] >= 0)
    allowed = same_segment & causal[None] | diagonal[None]
    return allowed[:, None, None, :, :]

def rotate(tensor, cosine, sine_table):
    half_size = tensor.shape[-1] // 2
    first_half = tensor[..., :half_size]
    second_half = tensor[..., half_size:]
    return jnp.concatenate([first_half * cosine - second_half * sine_table, second_half * cosine + first_half * sine_table], axis=-1)

def unrotate(tensor, cosine, sine_table):
    half_size = tensor.shape[-1] // 2
    first_half = tensor[..., :half_size]
    second_half = tensor[..., half_size:]
    return jnp.concatenate([first_half * cosine + second_half * sine_table, second_half * cosine - first_half * sine_table], axis=-1)

def batched(formula, left_side, right_side):
    return jnp.einsum(formula, left_side.astype(jnp.float32), right_side.astype(jnp.float32))

def project(left_side, weight):
    return jnp.dot(left_side, weight, preferred_element_type=jnp.float32)

def project_back(left_side, weight):
    return jnp.dot(left_side, weight.T, preferred_element_type=jnp.float32)

def attention_scores(query_rot, key_rot):
    return batched('gikrd,gjkd->gkrij', query_rot, key_rot) * HD ** (-0.5)

def block_pass(block_x, block_segments, block_cotangent, weights, attn_gain, mlp_gain):
    query_weight, key_weight, value_weight, out_weight, gate_weight, up_weight, down_weight = weights
    group_count, row_count = block_segments.shape
    all_rows = group_count * row_count
    cosine, sine_table = rotary_tables(block_segments)
    allowed = allowed_pairs(block_segments)
    root_attn = inverse_root(block_x)
    normed_attn = (block_x * root_attn * attn_gain).astype(jnp.bfloat16)
    query_proj = project(normed_attn, query_weight).reshape(group_count, row_count, H, HD)
    key_proj = project(normed_attn, key_weight).reshape(group_count, row_count, KV, HD)
    values = project(normed_attn, value_weight).astype(jnp.bfloat16).reshape(group_count, row_count, KV, HD)
    query_rot = rotate(query_proj, cosine, sine_table).astype(jnp.bfloat16).reshape(group_count, row_count, KV, GROUP, HD)
    key_rot = rotate(key_proj, cosine, sine_table).astype(jnp.bfloat16)
    scores = attention_scores(query_rot, key_rot)
    exp_total = lax.optimization_barrier(jnp.sum(jnp.where(allowed, jnp.exp(scores), 0.0), axis=-1, keepdims=True))
    log_total = jnp.log(exp_total)
    attn_probs = jnp.where(allowed, jnp.exp(scores - log_total), 0.0).astype(jnp.bfloat16)
    mixed_heads = batched('gkrij,gjkd->gikrd', attn_probs, values).astype(jnp.bfloat16).reshape(all_rows, D)
    hidden = block_x + project(mixed_heads, out_weight)
    root_mlp = inverse_root(hidden)
    normed_mlp = (hidden * root_mlp * mlp_gain).astype(jnp.bfloat16)
    gate_proj = project(normed_mlp, gate_weight)
    up_proj = project(normed_mlp, up_weight)
    sigmoid_gate = jax.nn.sigmoid(gate_proj)
    activation = (gate_proj * sigmoid_gate * up_proj).astype(jnp.bfloat16)
    output = hidden + project(activation, down_weight)
    live_rows = (block_segments.reshape(-1) >= 0).astype(jnp.float32)[:, None]
    grad_rows = block_cotangent * live_rows
    grad_rows_b = grad_rows.astype(jnp.bfloat16)
    grad_act = project_back(grad_rows_b, down_weight)
    grad_gate_b = (grad_act * up_proj * sigmoid_gate * (1.0 + gate_proj * (1.0 - sigmoid_gate))).astype(jnp.bfloat16)
    grad_up_b = (grad_act * gate_proj * sigmoid_gate).astype(jnp.bfloat16)
    grad_normed_mlp = project_back(grad_gate_b, gate_weight) + project_back(grad_up_b, up_weight)
    scaled_mlp = grad_normed_mlp * mlp_gain
    mlp_gain_term = lax.optimization_barrier(jnp.sum(grad_normed_mlp * hidden * root_mlp, axis=0))
    grad_hidden = grad_rows + root_mlp * scaled_mlp - hidden * root_mlp ** 3 * lax.optimization_barrier(jnp.mean(scaled_mlp * hidden, axis=-1, keepdims=True))
    grad_hidden_b = grad_hidden.astype(jnp.bfloat16)
    grad_mixed = project_back(grad_hidden_b, out_weight).astype(jnp.bfloat16).reshape(group_count, row_count, KV, GROUP, HD)
    probs_again = jnp.where(allowed, jnp.exp(attention_scores(query_rot, key_rot) - log_total), 0.0)
    grad_probs = batched('gikrd,gjkd->gkrij', grad_mixed, values)
    inner_sum = lax.optimization_barrier(jnp.sum(probs_again * grad_probs, axis=-1, keepdims=True))
    grad_scores = (probs_again * (grad_probs - inner_sum) * HD ** (-0.5)).astype(jnp.bfloat16)
    grad_q = batched('gkrij,gjkd->gikrd', grad_scores, key_rot).reshape(group_count, row_count, H, HD)
    grad_k = batched('gkrij,gikrd->gjkd', grad_scores, query_rot)
    grad_v = batched('gkrij,gikrd->gjkd', attn_probs, grad_mixed)
    grad_q_b = unrotate(grad_q, cosine, sine_table).astype(jnp.bfloat16).reshape(all_rows, D)
    grad_k_b = unrotate(grad_k, cosine, sine_table).astype(jnp.bfloat16).reshape(all_rows, KV * HD)
    grad_v_b = grad_v.astype(jnp.bfloat16).reshape(all_rows, KV * HD)
    grad_normed_attn = project_back(grad_q_b, query_weight) + project_back(grad_k_b, key_weight) + project_back(grad_v_b, value_weight)
    scaled_attn = grad_normed_attn * attn_gain
    attn_gain_term = lax.optimization_barrier(jnp.sum(grad_normed_attn * block_x * root_attn, axis=0))
    grad_input = grad_hidden + root_attn * scaled_attn - block_x * root_attn ** 3 * lax.optimization_barrier(jnp.mean(scaled_attn * block_x, axis=-1, keepdims=True))
    factors = ((normed_attn, grad_q_b), (normed_attn, grad_k_b), (normed_attn, grad_v_b), (mixed_heads, grad_hidden_b), (normed_mlp, grad_gate_b), (normed_mlp, grad_up_b), (activation, grad_rows_b))
    return (output, grad_input, factors, attn_gain_term, mlp_gain_term)

def reference(stream, segments, cotangent, attn_gain, mlp_gain, w_query, w_key, w_value, w_out, w_gate, w_up, w_down):
    matrix_shapes = ((D, D), (D, KV * HD), (D, KV * HD), (D, D), (D, FF), (D, FF), (FF, D))
    flat_list = (w_query, w_key, w_value, w_out, w_gate, w_up, w_down)
    weights = tuple((flat_piece.reshape(piece_shape) for flat_piece, piece_shape in zip(flat_list, matrix_shapes)))
    blocks = TOKENS // MB_ROWS
    per_step = math.gcd(blocks, 32)
    step_count = blocks // per_step
    x_steps = stream.reshape(step_count, per_step * MB_ROWS, D)
    segment_steps = segments.reshape(step_count, per_step, MB_ROWS)
    cotangent_steps = cotangent.reshape(step_count, per_step * MB_ROWS, D)
    initial = (tuple((jnp.zeros(piece_shape, jnp.float32) for piece_shape in matrix_shapes)), jnp.zeros((D,), jnp.float32), jnp.zeros((D,), jnp.float32))

    def scan_step(carried, sliced):
        weight_grads, attn_sum, mlp_sum = carried
        block_x, block_segments, block_cotangent = sliced
        block_out, block_dx, factors, attn_term, mlp_term = block_pass(block_x, block_segments, block_cotangent, weights, attn_gain, mlp_gain)
        weight_grads = tuple((grad_sum + jnp.dot(left_side.T, right_side, preferred_element_type=jnp.float32) for grad_sum, (left_side, right_side) in zip(weight_grads, factors)))
        return ((weight_grads, attn_sum + attn_term, mlp_sum + mlp_term), (block_out, block_dx))
    (weight_grads, attn_sum, mlp_sum), (out_steps, dx_steps) = lax.scan(scan_step, initial, (x_steps, segment_steps, cotangent_steps))
    flat_grads = tuple((grad_sum.reshape(-1) for grad_sum in weight_grads))
    return (out_steps.reshape(TOKENS, D), dx_steps.reshape(TOKENS, D), flat_grads[0], flat_grads[1], flat_grads[2], flat_grads[3], flat_grads[4], flat_grads[5], flat_grads[6], attn_sum, mlp_sum)
```

```python
import jax
import jax.numpy as jnp
from jax import lax
from jax.experimental import pallas as pl
from jax.experimental.pallas import tpu as pltpu
from jax.sharding import PartitionSpec as P
import functools

D = 960
H = 15
KV = 5
HD = 64
FF = 2560
MB_ROWS = 64
MBATCH = 2
GROUP = 3


EPSILON = 1e-05
ROPE_BASE = 10000.0


def inverse_root(values):
    return lax.rsqrt(jnp.mean(values * values, axis=-1, keepdims=True) + EPSILON)


def rotary_tables(block_segments):
    row_count = block_segments.shape[-1]
    row_index = jnp.arange(row_count)
    earlier = (block_segments[:, :, None] == block_segments[:, None, :]) & (
        row_index[None, None, :] < row_index[None, :, None]
    )
    position = jnp.sum(earlier.astype(jnp.float32), axis=-1)
    half_size = HD // 2
    frequency = ROPE_BASE ** (-2.0 * jnp.arange(half_size, dtype=jnp.float32) / HD)
    angle_table = position[:, :, None, None] * frequency
    return (jnp.cos(angle_table), jnp.sin(angle_table))


def allowed_pairs(block_segments):
    row_count = block_segments.shape[-1]
    row_index = jnp.arange(row_count)
    causal = row_index[None, :] <= row_index[:, None]
    diagonal = row_index[None, :] == row_index[:, None]
    same_segment = (block_segments[:, :, None] == block_segments[:, None, :]) & (
        block_segments[:, :, None] >= 0
    )
    allowed = same_segment & causal[None] | diagonal[None]
    return allowed[:, None, None, :, :]


def rotate(tensor, cosine, sine_table):
    half_size = tensor.shape[-1] // 2
    first_half = tensor[..., :half_size]
    second_half = tensor[..., half_size:]
    return jnp.concatenate(
        [
            first_half * cosine - second_half * sine_table,
            second_half * cosine + first_half * sine_table,
        ],
        axis=-1,
    )


def unrotate(tensor, cosine, sine_table):
    half_size = tensor.shape[-1] // 2
    first_half = tensor[..., :half_size]
    second_half = tensor[..., half_size:]
    return jnp.concatenate(
        [
            first_half * cosine + second_half * sine_table,
            second_half * cosine - first_half * sine_table,
        ],
        axis=-1,
    )


def batched(formula, left_side, right_side):
    return jnp.einsum(formula, left_side, right_side, preferred_element_type=jnp.float32)


def project(left_side, weight):
    return jnp.dot(left_side, weight, preferred_element_type=jnp.float32)


def project_back(left_side, weight):
    return lax.dot_general(
        left_side, weight, (((1,), (1,)), ((), ())), preferred_element_type=jnp.float32
    )


def outer_sum(left_side, right_side):
    return lax.dot_general(
        left_side, right_side, (((0,), (0,)), ((), ())), preferred_element_type=jnp.float32
    )


def attention_scores(query_rot, key_rot):
    return batched("gikrd,gjkd->gkrij", query_rot, key_rot) * HD ** (-0.5)


def owner_terms(factor_list, matrix_shapes, device_count):
    shard_sizes = [rows_m * cols_m // device_count for rows_m, cols_m in matrix_shapes]
    shard_total = sum(shard_sizes)

    def one_owner(owner):
        pieces = []
        for (left_side, right_side), (rows_m, cols_m), shard in zip(
            factor_list, matrix_shapes, shard_sizes
        ):
            span = min(rows_m, shard // cols_m + 2)
            offset = owner * shard
            row_first = jnp.minimum(offset // cols_m, rows_m - span)
            columns = lax.dynamic_slice_in_dim(left_side, row_first, span, 1)
            block = outer_sum(columns, right_side).reshape(-1)
            pieces.append(lax.dynamic_slice_in_dim(block, offset - row_first * cols_m, shard, 0))
        return jnp.concatenate(pieces)

    def term_rows(start, count):
        owners = count // shard_total
        owner_list = jnp.arange(owners, dtype=jnp.int32)
        return lax.map(one_owner, owner_list).reshape(-1)

    return (term_rows, shard_sizes, shard_total)


def split_shards(summed, shard_sizes):
    result = []
    begin = 0
    for shard in shard_sizes:
        result.append(summed[begin : begin + shard])
        begin = begin + shard
    return tuple(result)


def block_pass(
    block_x, block_segments, block_cotangent, forward_weights, fetch_weights, attn_gain, mlp_gain
):
    query_weight, key_weight, value_weight, out_weight, gate_weight, up_weight, down_weight = (
        forward_weights
    )
    group_count, row_count = block_segments.shape
    all_rows = group_count * row_count
    cosine, sine_table = rotary_tables(block_segments)
    allowed = allowed_pairs(block_segments)
    root_attn = inverse_root(block_x)
    normed_attn = (block_x * root_attn * attn_gain).astype(jnp.bfloat16)
    query_proj = project(normed_attn, query_weight).reshape(group_count, row_count, H, HD)
    key_proj = project(normed_attn, key_weight).reshape(group_count, row_count, KV, HD)
    values = (
        project(normed_attn, value_weight)
        .astype(jnp.bfloat16)
        .reshape(group_count, row_count, KV, HD)
    )
    query_rot = (
        rotate(query_proj, cosine, sine_table)
        .astype(jnp.bfloat16)
        .reshape(group_count, row_count, KV, GROUP, HD)
    )
    key_rot = rotate(key_proj, cosine, sine_table).astype(jnp.bfloat16)
    scores = attention_scores(query_rot, key_rot)
    exp_total = jnp.sum(jnp.where(allowed, jnp.exp(scores), 0.0), axis=-1, keepdims=True)
    log_total = jnp.log(exp_total)
    attn_probs = jnp.where(allowed, jnp.exp(scores - log_total), 0.0).astype(jnp.bfloat16)
    mixed_heads = (
        batched("gkrij,gjkd->gikrd", attn_probs, values).astype(jnp.bfloat16).reshape(all_rows, D)
    )
    hidden = block_x + project(mixed_heads, out_weight)
    root_mlp = inverse_root(hidden)
    normed_mlp = (hidden * root_mlp * mlp_gain).astype(jnp.bfloat16)
    gate_proj = project(normed_mlp, gate_weight)
    up_proj = project(normed_mlp, up_weight)
    sigmoid_gate = jax.nn.sigmoid(gate_proj)
    activation = (gate_proj * sigmoid_gate * up_proj).astype(jnp.bfloat16)
    output = hidden + project(activation, down_weight)
    query_weight, key_weight, value_weight, out_weight, gate_weight, up_weight, down_weight = (
        fetch_weights()
    )
    live_rows = (block_segments.reshape(-1) >= 0).astype(jnp.float32)[:, None]
    grad_rows = block_cotangent * live_rows
    grad_rows_b = grad_rows.astype(jnp.bfloat16)
    grad_act = project_back(grad_rows_b, down_weight)
    grad_gate_b = (
        grad_act * up_proj * sigmoid_gate * (1.0 + gate_proj * (1.0 - sigmoid_gate))
    ).astype(jnp.bfloat16)
    grad_up_b = (grad_act * gate_proj * sigmoid_gate).astype(jnp.bfloat16)
    grad_normed_mlp = project_back(grad_gate_b, gate_weight) + project_back(grad_up_b, up_weight)
    scaled_mlp = grad_normed_mlp * mlp_gain
    mlp_gain_term = jnp.sum(grad_normed_mlp * hidden * root_mlp, axis=0)
    grad_hidden = (
        grad_rows
        + root_mlp * scaled_mlp
        - hidden * root_mlp**3 * jnp.mean(scaled_mlp * hidden, axis=-1, keepdims=True)
    )
    grad_hidden_b = grad_hidden.astype(jnp.bfloat16)
    grad_mixed = (
        project_back(grad_hidden_b, out_weight)
        .astype(jnp.bfloat16)
        .reshape(group_count, row_count, KV, GROUP, HD)
    )
    probs_again = jnp.where(allowed, jnp.exp(attention_scores(query_rot, key_rot) - log_total), 0.0)
    grad_probs = batched("gikrd,gjkd->gkrij", grad_mixed, values)
    inner_sum = jnp.sum(probs_again * grad_probs, axis=-1, keepdims=True)
    grad_scores = (probs_again * (grad_probs - inner_sum) * HD ** (-0.5)).astype(jnp.bfloat16)
    grad_q = batched("gkrij,gjkd->gikrd", grad_scores, key_rot).reshape(
        group_count, row_count, H, HD
    )
    grad_k = batched("gkrij,gikrd->gjkd", grad_scores, query_rot)
    grad_v = batched("gkrij,gikrd->gjkd", attn_probs, grad_mixed)
    grad_q_b = unrotate(grad_q, cosine, sine_table).astype(jnp.bfloat16).reshape(all_rows, D)
    grad_k_b = unrotate(grad_k, cosine, sine_table).astype(jnp.bfloat16).reshape(all_rows, KV * HD)
    grad_v_b = grad_v.astype(jnp.bfloat16).reshape(all_rows, KV * HD)
    grad_normed_attn = (
        project_back(grad_q_b, query_weight)
        + project_back(grad_k_b, key_weight)
        + project_back(grad_v_b, value_weight)
    )
    scaled_attn = grad_normed_attn * attn_gain
    attn_gain_term = jnp.sum(grad_normed_attn * block_x * root_attn, axis=0)
    grad_input = (
        grad_hidden
        + root_attn * scaled_attn
        - block_x * root_attn**3 * jnp.mean(scaled_attn * block_x, axis=-1, keepdims=True)
    )
    factors = (
        (normed_attn, grad_q_b),
        (normed_attn, grad_k_b),
        (normed_attn, grad_v_b),
        (mixed_heads, grad_hidden_b),
        (normed_mlp, grad_gate_b),
        (normed_mlp, grad_up_b),
        (activation, grad_rows_b),
    )
    return (output, grad_input, factors, attn_gain_term, mlp_gain_term)


def local(
    stream,
    segments,
    cotangent,
    attn_gain,
    mlp_gain,
    w_query,
    w_key,
    w_value,
    w_out,
    w_gate,
    w_up,
    w_down,
):
    matrix_shapes = ((D, D), (D, KV * HD), (D, KV * HD), (D, D), (D, FF), (D, FF), (FF, D))
    device_count = lax.axis_size("dp")
    flat_list = (
        lax.all_gather(w_query, "dp", axis=0, tiled=True),
        lax.all_gather(w_key, "dp", axis=0, tiled=True),
        lax.all_gather(w_value, "dp", axis=0, tiled=True),
        lax.all_gather(w_out, "dp", axis=0, tiled=True),
        lax.all_gather(w_gate, "dp", axis=0, tiled=True),
        lax.all_gather(w_up, "dp", axis=0, tiled=True),
        lax.all_gather(w_down, "dp", axis=0, tiled=True),
    )
    kept_weights = tuple(
        (
            flat_piece.reshape(piece_shape)
            for flat_piece, piece_shape in zip(flat_list, matrix_shapes)
        )
    )
    block_outputs = []
    block_grads = []
    saved_factors = []
    owned_grads = None
    attn_sum = jnp.zeros((D,), jnp.float32)
    mlp_sum = jnp.zeros((D,), jnp.float32)
    for batch_index in range(MBATCH):
        first_row = batch_index * MB_ROWS
        block_x = stream[first_row : first_row + MB_ROWS]
        block_cotangent = cotangent[first_row : first_row + MB_ROWS]
        block_segments = segments[first_row : first_row + MB_ROWS].reshape(1, MB_ROWS)

        def fetch_weights():
            return kept_weights

        block_out, block_dx, factors, attn_term, mlp_term = block_pass(
            block_x,
            block_segments,
            block_cotangent,
            kept_weights,
            fetch_weights,
            attn_gain,
            mlp_gain,
        )
        block_outputs.append(block_out)
        block_grads.append(block_dx)
        attn_sum = attn_sum + attn_term
        mlp_sum = mlp_sum + mlp_term
        saved_factors.append(factors)
    joined = []
    for member in range(7):
        left_side = jnp.concatenate([record[member][0] for record in saved_factors], axis=0)
        right_side = jnp.concatenate([record[member][1] for record in saved_factors], axis=0)
        joined.append((left_side, right_side))
    term_rows, shard_sizes, shard_total = owner_terms(joined, matrix_shapes, device_count)
    owned_grads = split_shards(
        lax.psum_scatter(
            term_rows(jnp.int32(0), lax.axis_size("dp") * shard_total),
            "dp",
            scatter_dimension=0,
            tiled=True,
        ),
        shard_sizes,
    )
    attn_total, mlp_total = lax.psum((attn_sum, mlp_sum), "dp")
    output = jnp.concatenate(block_outputs, axis=0)
    grad_x = jnp.concatenate(block_grads, axis=0)
    return (
        output,
        grad_x,
        owned_grads[0],
        owned_grads[1],
        owned_grads[2],
        owned_grads[3],
        owned_grads[4],
        owned_grads[5],
        owned_grads[6],
        attn_total,
        mlp_total,
    )


MESH = pl.DeviceIdType.MESH


def ring_place(device, chips):
    depth = chips // 4
    chip = device // 2
    z, y, x = chip // 4, (chip // 2) % 2, chip % 2
    column = 2 * y + (x + y) % 2
    odd = column % 2
    along = z * (1 - odd) + (depth - 1 - z) * odd
    return column * depth + along


def ring_chip(place, chips):
    depth = chips // 4
    column, along = place // depth, place % depth
    odd = column % 2
    z = along * (1 - odd) + (depth - 1 - along) * odd
    y = column // 2
    x = (column + y) % 2
    return z * 4 + y * 2 + x


def neighbours(chips):
    me = lax.axis_index("dp")
    core = me % 2
    sign = 1 - 2 * core
    place = ring_place(me, chips)

    def owner_at(steps, parity, direction):
        spot = (place - direction * steps + 2 * chips) % chips
        return ring_chip(spot, chips) * 2 + parity

    partner = me + sign
    after = owner_at(-1, core, sign)
    before = owner_at(1, core, sign)
    return me, core, sign, partner, after, before, owner_at


def greet(devices):
    barrier = pltpu.get_barrier_semaphore()
    for device in devices:
        pl.semaphore_signal(barrier, inc=1, device_id=(device,), device_id_type=MESH)
    pl.semaphore_wait(barrier, len(devices))


def remote(source, target, send, recv, device):
    return pltpu.make_async_remote_copy(
        src_ref=source,
        dst_ref=target,
        send_sem=send,
        recv_sem=recv,
        device_id=(device,),
        device_id_type=MESH,
    )


def gather_kernel(
    chips, wide_ref, tall_ref, wide_out, tall_out, local_sem, ring_send, ring_recv, pair_send, pair_recv
):
    me, core, sign, partner, after, before, owner_at = neighbours(chips)
    greet((partner, after, before))
    half = wide_ref.shape[1] // 2

    def views(wide, tall):
        return (
            wide.at[:, pl.ds(0, half)],
            wide.at[:, pl.ds(half, half)],
            tall,
        )

    own = views(wide_ref, tall_ref)

    def slot(owner):
        return views(wide_out.at[owner], tall_out.at[owner])

    mine = slot(me)
    for piece in range(3):
        remote(
            own[piece], mine[piece], ring_send.at[piece, 0], ring_recv.at[piece, 0], after
        ).start()
    keep = [
        pltpu.make_async_copy(own[piece], mine[piece], local_sem.at[piece]) for piece in range(3)
    ]
    for piece in range(3):
        remote(
            own[piece], mine[piece], pair_send.at[piece, 0], pair_recv.at[piece, 0], partner
        ).start()
        keep[piece].start()

    def arrive(step, last):
        block = slot(owner_at(step, core, sign))
        for piece in range(3):
            remote(
                block[piece],
                block[piece],
                ring_send.at[piece, step - 1],
                ring_recv.at[piece, step - 1],
                after,
            ).wait_recv()
            if not last:
                remote(
                    block[piece],
                    block[piece],
                    ring_send.at[piece, step],
                    ring_recv.at[piece, step],
                    after,
                ).start()
            remote(
                block[piece],
                block[piece],
                pair_send.at[piece, step],
                pair_recv.at[piece, step],
                partner,
            ).start()

    @pl.loop(1, chips - 1)
    def _(step):
        arrive(step, False)

    arrive(chips - 1, True)

    @pl.loop(0, chips)
    def _(step):
        block = slot(owner_at(step, 1 - core, -sign))
        sent = slot(owner_at(step, core, sign))
        for piece in range(3):
            remote(
                sent[piece], sent[piece], pair_send.at[piece, step], pair_recv.at[piece, step], partner
            ).wait_send()
            remote(
                block[piece],
                block[piece],
                pair_send.at[piece, step],
                pair_recv.at[piece, step],
                partner,
            ).wait_recv()

    @pl.loop(0, chips - 1)
    def _(step):
        sent = slot(owner_at(step, core, sign))
        for piece in range(3):
            remote(
                sent[piece], sent[piece], ring_send.at[piece, step], ring_recv.at[piece, step], after
            ).wait_send()

    for piece in range(3):
        keep[piece].wait()


def gather_blocks(wide, tall, device_count):
    chips = device_count // 2
    moved = (wide.size + tall.size) * 2 * (device_count - 1)
    return pl.pallas_call(
        functools.partial(gather_kernel, chips),
        out_shape=(
            jax.ShapeDtypeStruct((device_count,) + wide.shape, wide.dtype),
            jax.ShapeDtypeStruct((device_count,) + tall.shape, tall.dtype),
        ),
        in_specs=[pl.BlockSpec(memory_space=pltpu.VMEM)] * 2,
        out_specs=(pl.BlockSpec(memory_space=pl.ANY),) * 2,
        scratch_shapes=[
            pltpu.SemaphoreType.DMA((3,)),
            pltpu.SemaphoreType.DMA((3, chips - 1)),
            pltpu.SemaphoreType.DMA((3, chips - 1)),
            pltpu.SemaphoreType.DMA((3, chips)),
            pltpu.SemaphoreType.DMA((3, chips)),
        ],
        compiler_params=pltpu.CompilerParams(collective_id=0, has_side_effects=True),
        cost_estimate=pl.CostEstimate(flops=0, bytes_accessed=10 * moved, transcendentals=0),
        name="gather_blocks",
    )(wide, tall)


def reduce_kernel(
    chips,
    wide_ref,
    tall_ref,
    wide_out,
    tall_out,
    wide_part,
    tall_part,
    wide_got,
    tall_got,
    ring_send,
    ring_recv,
    pair_send,
    pair_recv,
):
    me, core, sign, partner, after, before, owner_at = neighbours(chips)
    greet((partner, after, before))
    half = wide_ref.shape[2] // 2

    def views(wide, tall):
        return (
            wide.at[:, pl.ds(0, half)],
            wide.at[:, pl.ds(half, half)],
            tall,
        )

    def term(owner):
        return views(wide_ref.at[owner], tall_ref.at[owner])

    def part(step):
        return views(wide_part.at[step], tall_part.at[step])

    def got(step):
        return views(wide_got.at[step], tall_got.at[step])

    def pair_copy(step, piece):
        source = term(owner_at(step + 1, 1 - core, -sign))
        return remote(
            source[piece],
            part(step)[piece],
            pair_send.at[piece, step],
            pair_recv.at[piece, step],
            partner,
        )

    def ring_copy(step, piece):
        return remote(
            part(step)[piece],
            got(step)[piece],
            ring_send.at[piece, step],
            ring_recv.at[piece, step],
            after,
        )

    @pl.loop(0, chips)
    def _(step):
        for piece in range(3):
            pair_copy(step, piece).start()

    def total(step, piece, first):
        own = term(owner_at(step + 1, core, sign))[piece]
        pair_copy(step, piece).wait_recv()
        value = own[...].astype(jnp.float32) + part(step)[piece][...].astype(jnp.float32)
        if not first:
            ring_copy(step - 1, piece).wait_recv()
            value = value + got(step - 1)[piece][...].astype(jnp.float32)
        return value

    def advance(step, first):
        for piece in range(3):
            part(step)[piece][...] = total(step, piece, first).astype(jnp.bfloat16)
            ring_copy(step, piece).start()

    advance(0, True)

    @pl.loop(1, chips - 1)
    def _(step):
        advance(step, False)

    out = views(wide_out, tall_out)
    for piece in range(3):
        out[piece][...] = total(chips - 1, piece, False)

    @pl.loop(0, chips)
    def _(step):
        for piece in range(3):
            pair_copy(step, piece).wait_send()

    @pl.loop(0, chips - 1)
    def _(step):
        for piece in range(3):
            ring_copy(step, piece).wait_send()


def reduce_blocks(wide, tall, device_count):
    chips = device_count // 2
    moved = (wide.size + tall.size) * 2
    return pl.pallas_call(
        functools.partial(reduce_kernel, chips),
        out_shape=(
            jax.ShapeDtypeStruct(wide.shape[1:], jnp.float32),
            jax.ShapeDtypeStruct(tall.shape[1:], jnp.float32),
        ),
        in_specs=[pl.BlockSpec(memory_space=pltpu.VMEM)] * 2,
        out_specs=(pl.BlockSpec(memory_space=pltpu.VMEM),) * 2,
        scratch_shapes=[
            pltpu.VMEM((chips,) + wide.shape[1:], jnp.bfloat16),
            pltpu.VMEM((chips,) + tall.shape[1:], jnp.bfloat16),
            pltpu.VMEM((chips - 1,) + wide.shape[1:], jnp.bfloat16),
            pltpu.VMEM((chips - 1,) + tall.shape[1:], jnp.bfloat16),
            pltpu.SemaphoreType.DMA((3, chips - 1)),
            pltpu.SemaphoreType.DMA((3, chips - 1)),
            pltpu.SemaphoreType.DMA((3, chips)),
            pltpu.SemaphoreType.DMA((3, chips)),
        ],
        compiler_params=pltpu.CompilerParams(
            collective_id=1, has_side_effects=True, vmem_limit_bytes=60 * 1024 * 1024
        ),
        cost_estimate=pl.CostEstimate(flops=0, bytes_accessed=10 * moved, transcendentals=0),
        name="reduce_blocks",
    )(wide, tall)


USE_KERNELS = True


def local_blocks(
    stream, segments, cotangent, attn_gain, mlp_gain, w_query, w_key, w_value, w_out, w_gate, w_up, w_down
):
    device_count = lax.axis_size("dp")
    rows = D // device_count
    tall_rows = FF // device_count
    padded = -(-rows // 16) * 16
    kv = KV * HD
    wide = jnp.concatenate(
        [
            w_query.reshape(rows, D),
            w_key.reshape(rows, kv),
            w_value.reshape(rows, kv),
            w_out.reshape(rows, D),
            w_gate.reshape(rows, FF),
            w_up.reshape(rows, FF),
        ],
        axis=1,
    )
    wide = jnp.pad(wide, ((0, padded - rows), (0, 0)))
    tall = w_down.reshape(tall_rows, D)
    if USE_KERNELS:
        wide_all, tall_all = gather_blocks(wide, tall, device_count)
    else:
        wide_all = lax.all_gather(wide, "dp", axis=0)
        tall_all = lax.all_gather(tall, "dp", axis=0)
    spread = device_count * padded
    wide_all = wide_all.reshape(spread, wide.shape[1])
    down_weight = tall_all.reshape(FF, D)
    qkv_width = D + 2 * kv
    qkv_weight = wide_all[:, :qkv_width]
    out_weight = wide_all[:, qkv_width : qkv_width + D]
    gate_up_weight = wide_all[:, qkv_width + D :]

    source = lax.broadcasted_iota(jnp.int32, (D, spread), 0)
    target = lax.broadcasted_iota(jnp.int32, (D, spread), 1)
    placing = (source // rows) * padded + source % rows == target

    def place(value):
        return project(value, placing.astype(jnp.bfloat16)).astype(jnp.bfloat16)

    def unplace(value):
        return lax.dot_general(
            value,
            placing.astype(jnp.float32),
            (((1,), (1,)), ((), ())),
            precision=lax.Precision.HIGHEST,
            preferred_element_type=jnp.float32,
        )

    def unplace_b(value):
        return project_back(value, placing.astype(jnp.bfloat16)).astype(jnp.bfloat16)

    row_total = stream.shape[0]
    groups = row_total // MB_ROWS
    block_segments = segments.reshape(groups, MB_ROWS)
    cosine, sine_table = rotary_tables(block_segments)
    allowed = allowed_pairs(block_segments)
    root_attn = inverse_root(stream)
    normed_attn = place((stream * root_attn * attn_gain).astype(jnp.bfloat16))
    qkv = project(normed_attn, qkv_weight)
    query_proj = qkv[:, :D].reshape(groups, MB_ROWS, H, HD)
    key_proj = qkv[:, D : D + kv].reshape(groups, MB_ROWS, KV, HD)
    values = qkv[:, D + kv :].astype(jnp.bfloat16).reshape(groups, MB_ROWS, KV, HD)
    query_rot = (
        rotate(query_proj, cosine, sine_table)
        .astype(jnp.bfloat16)
        .reshape(groups, MB_ROWS, KV, GROUP, HD)
    )
    key_rot = rotate(key_proj, cosine, sine_table).astype(jnp.bfloat16)
    scores = attention_scores(query_rot, key_rot)
    exp_total = jnp.sum(jnp.where(allowed, jnp.exp(scores), 0.0), axis=-1, keepdims=True)
    log_total = jnp.log(exp_total)
    probs = jnp.where(allowed, jnp.exp(scores - log_total), 0.0)
    attn_probs = probs.astype(jnp.bfloat16)
    mixed_heads = place(
        batched("gkrij,gjkd->gikrd", attn_probs, values).astype(jnp.bfloat16).reshape(row_total, D)
    )
    hidden = stream + project(mixed_heads, out_weight)
    root_mlp = inverse_root(hidden)
    normed_mlp = place((hidden * root_mlp * mlp_gain).astype(jnp.bfloat16))
    gate_up = project(normed_mlp, gate_up_weight)
    gate_proj = gate_up[:, :FF]
    up_proj = gate_up[:, FF:]
    sigmoid_gate = jax.nn.sigmoid(gate_proj)
    activation = (gate_proj * sigmoid_gate * up_proj).astype(jnp.bfloat16)
    output = hidden + project(activation, down_weight)

    live_rows = (segments >= 0).astype(jnp.float32)[:, None]
    grad_rows = cotangent * live_rows
    grad_rows_b = grad_rows.astype(jnp.bfloat16)
    grad_act = project_back(grad_rows_b, down_weight)
    grad_gate_b = (
        grad_act * up_proj * sigmoid_gate * (1.0 + gate_proj * (1.0 - sigmoid_gate))
    ).astype(jnp.bfloat16)
    grad_up_b = (grad_act * gate_proj * sigmoid_gate).astype(jnp.bfloat16)
    grad_gate_up = jnp.concatenate([grad_gate_b, grad_up_b], axis=1)
    grad_normed_mlp = unplace(project_back(grad_gate_up, gate_up_weight))
    scaled_mlp = grad_normed_mlp * mlp_gain
    mlp_gain_term = jnp.sum(grad_normed_mlp * hidden * root_mlp, axis=0)
    grad_hidden = (
        grad_rows
        + root_mlp * scaled_mlp
        - hidden * root_mlp**3 * jnp.mean(scaled_mlp * hidden, axis=-1, keepdims=True)
    )
    grad_hidden_b = grad_hidden.astype(jnp.bfloat16)
    grad_mixed = unplace_b(
        project_back(grad_hidden_b, out_weight).astype(jnp.bfloat16)
    ).reshape(groups, MB_ROWS, KV, GROUP, HD)
    grad_probs = batched("gikrd,gjkd->gkrij", grad_mixed, values)
    inner_sum = jnp.sum(probs * grad_probs, axis=-1, keepdims=True)
    grad_scores = (probs * (grad_probs - inner_sum) * HD ** (-0.5)).astype(jnp.bfloat16)
    grad_q = batched("gkrij,gjkd->gikrd", grad_scores, key_rot).reshape(groups, MB_ROWS, H, HD)
    grad_k = batched("gkrij,gikrd->gjkd", grad_scores, query_rot)
    grad_v = batched("gkrij,gikrd->gjkd", attn_probs, grad_mixed)
    grad_qkv = jnp.concatenate(
        [
            unrotate(grad_q, cosine, sine_table).astype(jnp.bfloat16).reshape(row_total, D),
            unrotate(grad_k, cosine, sine_table).astype(jnp.bfloat16).reshape(row_total, kv),
            grad_v.astype(jnp.bfloat16).reshape(row_total, kv),
        ],
        axis=1,
    )
    grad_normed_attn = unplace(project_back(grad_qkv, qkv_weight))
    scaled_attn = grad_normed_attn * attn_gain
    attn_gain_term = jnp.sum(grad_normed_attn * stream * root_attn, axis=0)
    grad_x = (
        grad_hidden
        + root_attn * scaled_attn
        - stream * root_attn**3 * jnp.mean(scaled_attn * stream, axis=-1, keepdims=True)
    )
    gain_terms = jnp.stack([attn_gain_term, mlp_gain_term])
    gain_total = jnp.sum(lax.all_gather(gain_terms, "dp", axis=0), axis=0)

    wide_terms = jnp.concatenate(
        [
            outer_sum(normed_attn, grad_qkv).astype(jnp.bfloat16),
            outer_sum(mixed_heads, grad_hidden_b).astype(jnp.bfloat16),
            outer_sum(normed_mlp, grad_gate_up).astype(jnp.bfloat16),
        ],
        axis=1,
    ).reshape(device_count, padded, wide.shape[1])
    tall_terms = (
        outer_sum(activation, grad_rows_b).astype(jnp.bfloat16).reshape(device_count, tall_rows, D)
    )
    if USE_KERNELS:
        wide_sum, tall_sum = reduce_blocks(wide_terms, tall_terms, device_count)
    else:
        wide_sum = lax.psum_scatter(wide_terms, "dp", scatter_dimension=0)
        tall_sum = lax.psum_scatter(tall_terms, "dp", scatter_dimension=0)
    wide_sum = wide_sum.astype(jnp.float32)[:rows]
    grads = []
    begin = 0
    for width in (D, kv, kv, D, FF, FF):
        grads.append(wide_sum[:, begin : begin + width].reshape(-1))
        begin += width
    grads.append(tall_sum.astype(jnp.float32).reshape(-1))
    return (output, grad_x, *grads, gain_total[0], gain_total[1])


def solution(mesh):
    device_count = mesh.shape["dp"]
    aligned = D % device_count == 0 and FF % device_count == 0 and device_count % 8 == 0
    body = local_blocks if aligned and device_count >= 16 else local
    placed = (
        P("dp", None),
        P("dp"),
        P("dp", None),
        P(),
        P(),
        P("dp"),
        P("dp"),
        P("dp"),
        P("dp"),
        P("dp"),
        P("dp"),
        P("dp"),
    )
    return jax.shard_map(
        body,
        mesh=mesh,
        in_specs=placed,
        out_specs=(
            P("dp", None),
            P("dp", None),
            P("dp"),
            P("dp"),
            P("dp"),
            P("dp"),
            P("dp"),
            P("dp"),
            P("dp"),
            P(),
            P(),
        ),
        check_vma=False,
    )
```

```python
import jax
import jax.numpy as jnp
from jax import lax
from jax.experimental import pallas as pl
from jax.experimental.pallas import tpu as pltpu
from jax.sharding import PartitionSpec as P
import functools

D = 960
H = 15
KV = 5
HD = 64
FF = 2560
MB_ROWS = 64
MBATCH = 2
GROUP = 3


EPSILON = 1e-05
ROPE_BASE = 10000.0


def inverse_root(values):
    return lax.rsqrt(jnp.mean(values * values, axis=-1, keepdims=True) + EPSILON)


def rotary_tables(block_segments):
    row_count = block_segments.shape[-1]
    row_index = jnp.arange(row_count)
    earlier = (block_segments[:, :, None] == block_segments[:, None, :]) & (
        row_index[None, None, :] < row_index[None, :, None]
    )
    position = jnp.sum(earlier.astype(jnp.float32), axis=-1)
    half_size = HD // 2
    frequency = ROPE_BASE ** (-2.0 * jnp.arange(half_size, dtype=jnp.float32) / HD)
    angle_table = position[:, :, None, None] * frequency
    return (jnp.cos(angle_table), jnp.sin(angle_table))


def allowed_pairs(block_segments):
    row_count = block_segments.shape[-1]
    row_index = jnp.arange(row_count)
    causal = row_index[None, :] <= row_index[:, None]
    diagonal = row_index[None, :] == row_index[:, None]
    same_segment = (block_segments[:, :, None] == block_segments[:, None, :]) & (
        block_segments[:, :, None] >= 0
    )
    allowed = same_segment & causal[None] | diagonal[None]
    return allowed[:, None, None, :, :]


def rotate(tensor, cosine, sine_table):
    half_size = tensor.shape[-1] // 2
    first_half = tensor[..., :half_size]
    second_half = tensor[..., half_size:]
    return jnp.concatenate(
        [
            first_half * cosine - second_half * sine_table,
            second_half * cosine + first_half * sine_table,
        ],
        axis=-1,
    )


def unrotate(tensor, cosine, sine_table):
    half_size = tensor.shape[-1] // 2
    first_half = tensor[..., :half_size]
    second_half = tensor[..., half_size:]
    return jnp.concatenate(
        [
            first_half * cosine + second_half * sine_table,
            second_half * cosine - first_half * sine_table,
        ],
        axis=-1,
    )


def batched(formula, left_side, right_side):
    return jnp.einsum(formula, left_side, right_side, preferred_element_type=jnp.float32)


def project(left_side, weight):
    return jnp.dot(left_side, weight, preferred_element_type=jnp.float32)


def project_back(left_side, weight):
    return lax.dot_general(
        left_side, weight, (((1,), (1,)), ((), ())), preferred_element_type=jnp.float32
    )


def outer_sum(left_side, right_side):
    return lax.dot_general(
        left_side, right_side, (((0,), (0,)), ((), ())), preferred_element_type=jnp.float32
    )


def attention_scores(query_rot, key_rot):
    return batched("gikrd,gjkd->gkrij", query_rot, key_rot) * HD ** (-0.5)


def owner_terms(factor_list, matrix_shapes, device_count):
    shard_sizes = [rows_m * cols_m // device_count for rows_m, cols_m in matrix_shapes]
    shard_total = sum(shard_sizes)

    def one_owner(owner):
        pieces = []
        for (left_side, right_side), (rows_m, cols_m), shard in zip(
            factor_list, matrix_shapes, shard_sizes
        ):
            span = min(rows_m, shard // cols_m + 2)
            offset = owner * shard
            row_first = jnp.minimum(offset // cols_m, rows_m - span)
            columns = lax.dynamic_slice_in_dim(left_side, row_first, span, 1)
            block = outer_sum(columns, right_side).reshape(-1)
            pieces.append(lax.dynamic_slice_in_dim(block, offset - row_first * cols_m, shard, 0))
        return jnp.concatenate(pieces)

    def term_rows(start, count):
        owners = count // shard_total
        owner_list = jnp.arange(owners, dtype=jnp.int32)
        return lax.map(one_owner, owner_list).reshape(-1)

    return (term_rows, shard_sizes, shard_total)


def split_shards(summed, shard_sizes):
    result = []
    begin = 0
    for shard in shard_sizes:
        result.append(summed[begin : begin + shard])
        begin = begin + shard
    return tuple(result)


def block_pass(
    block_x, block_segments, block_cotangent, forward_weights, fetch_weights, attn_gain, mlp_gain
):
    query_weight, key_weight, value_weight, out_weight, gate_weight, up_weight, down_weight = (
        forward_weights
    )
    group_count, row_count = block_segments.shape
    all_rows = group_count * row_count
    cosine, sine_table = rotary_tables(block_segments)
    allowed = allowed_pairs(block_segments)
    root_attn = inverse_root(block_x)
    normed_attn = (block_x * root_attn * attn_gain).astype(jnp.bfloat16)
    query_proj = project(normed_attn, query_weight).reshape(group_count, row_count, H, HD)
    key_proj = project(normed_attn, key_weight).reshape(group_count, row_count, KV, HD)
    values = (
        project(normed_attn, value_weight)
        .astype(jnp.bfloat16)
        .reshape(group_count, row_count, KV, HD)
    )
    query_rot = (
        rotate(query_proj, cosine, sine_table)
        .astype(jnp.bfloat16)
        .reshape(group_count, row_count, KV, GROUP, HD)
    )
    key_rot = rotate(key_proj, cosine, sine_table).astype(jnp.bfloat16)
    scores = attention_scores(query_rot, key_rot)
    exp_total = jnp.sum(jnp.where(allowed, jnp.exp(scores), 0.0), axis=-1, keepdims=True)
    log_total = jnp.log(exp_total)
    attn_probs = jnp.where(allowed, jnp.exp(scores - log_total), 0.0).astype(jnp.bfloat16)
    mixed_heads = (
        batched("gkrij,gjkd->gikrd", attn_probs, values).astype(jnp.bfloat16).reshape(all_rows, D)
    )
    hidden = block_x + project(mixed_heads, out_weight)
    root_mlp = inverse_root(hidden)
    normed_mlp = (hidden * root_mlp * mlp_gain).astype(jnp.bfloat16)
    gate_proj = project(normed_mlp, gate_weight)
    up_proj = project(normed_mlp, up_weight)
    sigmoid_gate = jax.nn.sigmoid(gate_proj)
    activation = (gate_proj * sigmoid_gate * up_proj).astype(jnp.bfloat16)
    output = hidden + project(activation, down_weight)
    query_weight, key_weight, value_weight, out_weight, gate_weight, up_weight, down_weight = (
        fetch_weights()
    )
    live_rows = (block_segments.reshape(-1) >= 0).astype(jnp.float32)[:, None]
    grad_rows = block_cotangent * live_rows
    grad_rows_b = grad_rows.astype(jnp.bfloat16)
    grad_act = project_back(grad_rows_b, down_weight)
    grad_gate_b = (
        grad_act * up_proj * sigmoid_gate * (1.0 + gate_proj * (1.0 - sigmoid_gate))
    ).astype(jnp.bfloat16)
    grad_up_b = (grad_act * gate_proj * sigmoid_gate).astype(jnp.bfloat16)
    grad_normed_mlp = project_back(grad_gate_b, gate_weight) + project_back(grad_up_b, up_weight)
    scaled_mlp = grad_normed_mlp * mlp_gain
    mlp_gain_term = jnp.sum(grad_normed_mlp * hidden * root_mlp, axis=0)
    grad_hidden = (
        grad_rows
        + root_mlp * scaled_mlp
        - hidden * root_mlp**3 * jnp.mean(scaled_mlp * hidden, axis=-1, keepdims=True)
    )
    grad_hidden_b = grad_hidden.astype(jnp.bfloat16)
    grad_mixed = (
        project_back(grad_hidden_b, out_weight)
        .astype(jnp.bfloat16)
        .reshape(group_count, row_count, KV, GROUP, HD)
    )
    probs_again = jnp.where(allowed, jnp.exp(attention_scores(query_rot, key_rot) - log_total), 0.0)
    grad_probs = batched("gikrd,gjkd->gkrij", grad_mixed, values)
    inner_sum = jnp.sum(probs_again * grad_probs, axis=-1, keepdims=True)
    grad_scores = (probs_again * (grad_probs - inner_sum) * HD ** (-0.5)).astype(jnp.bfloat16)
    grad_q = batched("gkrij,gjkd->gikrd", grad_scores, key_rot).reshape(
        group_count, row_count, H, HD
    )
    grad_k = batched("gkrij,gikrd->gjkd", grad_scores, query_rot)
    grad_v = batched("gkrij,gikrd->gjkd", attn_probs, grad_mixed)
    grad_q_b = unrotate(grad_q, cosine, sine_table).astype(jnp.bfloat16).reshape(all_rows, D)
    grad_k_b = unrotate(grad_k, cosine, sine_table).astype(jnp.bfloat16).reshape(all_rows, KV * HD)
    grad_v_b = grad_v.astype(jnp.bfloat16).reshape(all_rows, KV * HD)
    grad_normed_attn = (
        project_back(grad_q_b, query_weight)
        + project_back(grad_k_b, key_weight)
        + project_back(grad_v_b, value_weight)
    )
    scaled_attn = grad_normed_attn * attn_gain
    attn_gain_term = jnp.sum(grad_normed_attn * block_x * root_attn, axis=0)
    grad_input = (
        grad_hidden
        + root_attn * scaled_attn
        - block_x * root_attn**3 * jnp.mean(scaled_attn * block_x, axis=-1, keepdims=True)
    )
    factors = (
        (normed_attn, grad_q_b),
        (normed_attn, grad_k_b),
        (normed_attn, grad_v_b),
        (mixed_heads, grad_hidden_b),
        (normed_mlp, grad_gate_b),
        (normed_mlp, grad_up_b),
        (activation, grad_rows_b),
    )
    return (output, grad_input, factors, attn_gain_term, mlp_gain_term)


def local(
    stream,
    segments,
    cotangent,
    attn_gain,
    mlp_gain,
    w_query,
    w_key,
    w_value,
    w_out,
    w_gate,
    w_up,
    w_down,
):
    matrix_shapes = ((D, D), (D, KV * HD), (D, KV * HD), (D, D), (D, FF), (D, FF), (FF, D))
    device_count = lax.axis_size("dp")
    flat_list = (
        lax.all_gather(w_query, "dp", axis=0, tiled=True),
        lax.all_gather(w_key, "dp", axis=0, tiled=True),
        lax.all_gather(w_value, "dp", axis=0, tiled=True),
        lax.all_gather(w_out, "dp", axis=0, tiled=True),
        lax.all_gather(w_gate, "dp", axis=0, tiled=True),
        lax.all_gather(w_up, "dp", axis=0, tiled=True),
        lax.all_gather(w_down, "dp", axis=0, tiled=True),
    )
    kept_weights = tuple(
        (
            flat_piece.reshape(piece_shape)
            for flat_piece, piece_shape in zip(flat_list, matrix_shapes)
        )
    )
    block_outputs = []
    block_grads = []
    saved_factors = []
    owned_grads = None
    attn_sum = jnp.zeros((D,), jnp.float32)
    mlp_sum = jnp.zeros((D,), jnp.float32)
    for batch_index in range(MBATCH):
        first_row = batch_index * MB_ROWS
        block_x = stream[first_row : first_row + MB_ROWS]
        block_cotangent = cotangent[first_row : first_row + MB_ROWS]
        block_segments = segments[first_row : first_row + MB_ROWS].reshape(1, MB_ROWS)

        def fetch_weights():
            return kept_weights

        block_out, block_dx, factors, attn_term, mlp_term = block_pass(
            block_x,
            block_segments,
            block_cotangent,
            kept_weights,
            fetch_weights,
            attn_gain,
            mlp_gain,
        )
        block_outputs.append(block_out)
        block_grads.append(block_dx)
        attn_sum = attn_sum + attn_term
        mlp_sum = mlp_sum + mlp_term
        saved_factors.append(factors)
    joined = []
    for member in range(7):
        left_side = jnp.concatenate([record[member][0] for record in saved_factors], axis=0)
        right_side = jnp.concatenate([record[member][1] for record in saved_factors], axis=0)
        joined.append((left_side, right_side))
    term_rows, shard_sizes, shard_total = owner_terms(joined, matrix_shapes, device_count)
    owned_grads = split_shards(
        lax.psum_scatter(
            term_rows(jnp.int32(0), lax.axis_size("dp") * shard_total),
            "dp",
            scatter_dimension=0,
            tiled=True,
        ),
        shard_sizes,
    )
    attn_total, mlp_total = lax.psum((attn_sum, mlp_sum), "dp")
    output = jnp.concatenate(block_outputs, axis=0)
    grad_x = jnp.concatenate(block_grads, axis=0)
    return (
        output,
        grad_x,
        owned_grads[0],
        owned_grads[1],
        owned_grads[2],
        owned_grads[3],
        owned_grads[4],
        owned_grads[5],
        owned_grads[6],
        attn_total,
        mlp_total,
    )


MESH = pl.DeviceIdType.MESH


def ring_place(device, chips):
    depth = chips // 4
    chip = device // 2
    z, y, x = chip // 4, (chip // 2) % 2, chip % 2
    column = 2 * y + (x + y) % 2
    odd = column % 2
    along = z * (1 - odd) + (depth - 1 - z) * odd
    return column * depth + along


def ring_chip(place, chips):
    depth = chips // 4
    column, along = place // depth, place % depth
    odd = column % 2
    z = along * (1 - odd) + (depth - 1 - along) * odd
    y = column // 2
    x = (column + y) % 2
    return z * 4 + y * 2 + x


def neighbours(chips):
    me = lax.axis_index("dp")
    core = me % 2
    sign = 1 - 2 * core
    place = ring_place(me, chips)

    def owner_at(steps, parity, direction):
        spot = (place - direction * steps + 2 * chips) % chips
        return ring_chip(spot, chips) * 2 + parity

    partner = me + sign
    after = owner_at(-1, core, sign)
    before = owner_at(1, core, sign)
    return me, core, sign, partner, after, before, owner_at


def greet(devices):
    barrier = pltpu.get_barrier_semaphore()
    for device in devices:
        pl.semaphore_signal(barrier, inc=1, device_id=(device,), device_id_type=MESH)
    pl.semaphore_wait(barrier, len(devices))


def remote(source, target, send, recv, device):
    return pltpu.make_async_remote_copy(
        src_ref=source,
        dst_ref=target,
        send_sem=send,
        recv_sem=recv,
        device_id=(device,),
        device_id_type=MESH,
    )


def gather_kernel(chips, count, *refs):
    own = refs[:count]
    gathered = refs[count : 2 * count]
    local_sem, ring_send, ring_recv, pair_send, pair_recv = refs[2 * count :]
    me, core, sign, partner, after, before, owner_at = neighbours(chips)
    greet((partner, after, before))

    def ring_copy(step, piece):
        block = gathered[piece].at[owner_at(step, core, sign)]
        source = own[piece] if isinstance(step, int) and step == 0 else block
        return remote(
            source, block, ring_send.at[piece, step], ring_recv.at[piece, step], after
        )

    def pair_copy(step, piece):
        block = gathered[piece].at[owner_at(step, core, sign)]
        source = own[piece] if isinstance(step, int) and step == 0 else block
        return remote(
            source, block, pair_send.at[piece, step], pair_recv.at[piece, step], partner
        )

    keep = [
        pltpu.make_async_copy(own[piece], gathered[piece].at[me], local_sem.at[piece])
        for piece in range(count)
    ]
    for piece in range(count):
        ring_copy(0, piece).start()
    for piece in range(count):
        pair_copy(0, piece).start()
        keep[piece].start()

    def arrive(step, last):
        for piece in range(count):
            block = gathered[piece].at[owner_at(step, core, sign)]
            remote(
                block, block, ring_send.at[piece, step - 1], ring_recv.at[piece, step - 1], after
            ).wait_recv()
            if not last:
                ring_copy(step, piece).start()
            pair_copy(step, piece).start()

    @pl.loop(1, chips - 1)
    def _(step):
        arrive(step, False)

    arrive(chips - 1, True)

    @pl.loop(0, chips)
    def _(step):
        for piece in range(count):
            block = gathered[piece].at[owner_at(step, 1 - core, -sign)]
            pair_copy(step, piece).wait_send()
            remote(
                block, block, pair_send.at[piece, step], pair_recv.at[piece, step], partner
            ).wait_recv()

    @pl.loop(0, chips - 1)
    def _(step):
        for piece in range(count):
            ring_copy(step, piece).wait_send()

    for piece in range(count):
        keep[piece].wait()


def gather_blocks(blocks, device_count):
    chips = device_count // 2
    count = len(blocks)
    moved = sum(block.size for block in blocks) * 2 * (device_count - 1)
    return pl.pallas_call(
        functools.partial(gather_kernel, chips, count),
        out_shape=tuple(
            jax.ShapeDtypeStruct((device_count,) + block.shape, block.dtype) for block in blocks
        ),
        in_specs=[pl.BlockSpec(memory_space=pltpu.VMEM)] * count,
        out_specs=(pl.BlockSpec(memory_space=pl.ANY),) * count,
        scratch_shapes=[
            pltpu.SemaphoreType.DMA((count,)),
            pltpu.SemaphoreType.DMA((count, chips - 1)),
            pltpu.SemaphoreType.DMA((count, chips - 1)),
            pltpu.SemaphoreType.DMA((count, chips)),
            pltpu.SemaphoreType.DMA((count, chips)),
        ],
        compiler_params=pltpu.CompilerParams(collective_id=0, has_side_effects=True),
        cost_estimate=pl.CostEstimate(flops=0, bytes_accessed=10 * moved, transcendentals=0),
        name="gather_blocks",
    )(*blocks)


def reduce_kernel(chips, count, *refs):
    lefts = refs[:count]
    rights = refs[count : 2 * count]
    gain_ref = refs[2 * count]
    refs = refs[2 * count + 1 :]
    outs = refs[:count]
    gain_out = refs[count]
    refs = refs[count + 1 :]
    terms = refs[:count]
    parts = refs[count : 2 * count]
    gots = refs[2 * count : 3 * count]
    gain_pair, gain_all = refs[3 * count : 3 * count + 2]
    ring_send, ring_recv, pair_send, pair_recv, gain_send, gain_recv = refs[3 * count + 2 :]
    me, core, sign, partner, after, before, owner_at = neighbours(chips)
    spot = ring_place(me, chips)
    greet((partner, after, before))

    def pair_copy(step, piece):
        return remote(
            terms[piece].at[owner_at(step + 1, 1 - core, -sign)],
            parts[piece].at[step],
            pair_send.at[piece, step],
            pair_recv.at[piece, step],
            partner,
        )

    def ring_copy(step, piece):
        return remote(
            parts[piece].at[step],
            gots[piece].at[step],
            ring_send.at[piece, step],
            ring_recv.at[piece, step],
            after,
        )

    gain_swap = remote(
        gain_ref, gain_pair, gain_send.at[chips - 1], gain_recv.at[chips - 1], partner
    )
    gain_swap.start()

    def gain_copy(step):
        held = gain_all.at[(spot - sign * step + 2 * chips) % chips]
        return remote(held, held, gain_send.at[step], gain_recv.at[step], after)

    def gain_arrived(step):
        held = gain_all.at[(spot - sign * (step + 1) + 2 * chips) % chips]
        return remote(held, held, gain_send.at[step], gain_recv.at[step], after)

    def multiply(piece):
        term, left, right = terms[piece], lefts[piece], rights[piece]
        owners, rows, width = term.shape
        if width % 512 == 0:

            @pl.loop(0, width // 512)
            def _(tile):
                columns = pl.ds(pl.multiple_of(tile * 512, 512), 512)
                block = jnp.dot(
                    left[...], right[:, columns], preferred_element_type=jnp.float32
                ).astype(jnp.bfloat16)
                term[:, :, columns] = block.reshape(owners, rows, 512)

        else:
            some = owners // 8

            @pl.loop(0, 8)
            def _(tile):
                spans = pl.ds(pl.multiple_of(tile * some * rows, some * rows), some * rows)
                block = jnp.dot(
                    left[spans, :], right[...], preferred_element_type=jnp.float32
                ).astype(jnp.bfloat16)
                term[pl.ds(tile * some, some)] = block.reshape(some, rows, width)

        @pl.loop(0, chips)
        def _(step):
            pair_copy(step, piece).start()

    def total(step, piece, first):
        pair_copy(step, piece).wait_recv()
        own = terms[piece][owner_at(step + 1, core, sign)]
        value = own.astype(jnp.float32) + parts[piece][step].astype(jnp.float32)
        if not first:
            ring_copy(step - 1, piece).wait_recv()
            value = value + gots[piece][step - 1].astype(jnp.float32)
        return value

    def advance(step, piece, first):
        parts[piece][step] = total(step, piece, first).astype(jnp.bfloat16)
        ring_copy(step, piece).start()

    for piece in range(count):
        multiply(piece)
        if piece == 0:
            gain_swap.wait_recv()
            gain_all[spot] = gain_ref[...] + gain_pair[...]
            gain_copy(0).start()
        else:
            advance(0, piece - 1, True)
    advance(0, count - 1, True)

    @pl.loop(1, chips - 1)
    def _(step):
        gain_arrived(step - 1).wait_recv()
        gain_copy(step).start()
        for piece in range(count):
            advance(step, piece, False)

    gain_arrived(chips - 2).wait_recv()
    gain_total = gain_all[0]
    for place in range(1, chips):
        gain_total = gain_total + gain_all[place]
    gain_out[...] = gain_total
    for piece in range(count):
        outs[piece][...] = total(chips - 1, piece, False)

    gain_swap.wait_send()

    @pl.loop(0, chips)
    def _(step):
        for piece in range(count):
            pair_copy(step, piece).wait_send()

    @pl.loop(0, chips - 1)
    def _(step):
        gain_copy(step).wait_send()
        for piece in range(count):
            ring_copy(step, piece).wait_send()


def reduce_blocks(lefts, rights, gains, device_count):
    chips = device_count // 2
    count = len(lefts)
    shapes = [
        (left.shape[0] // device_count, right.shape[1]) for left, right in zip(lefts, rights)
    ]
    sizes = [rows * width for rows, width in shapes]
    flops = sum(2 * left.size * right.shape[1] for left, right in zip(lefts, rights))
    vmem = pl.BlockSpec(memory_space=pltpu.VMEM)
    return pl.pallas_call(
        functools.partial(reduce_kernel, chips, count),
        out_shape=tuple(jax.ShapeDtypeStruct(shape, jnp.float32) for shape in shapes)
        + (jax.ShapeDtypeStruct(gains.shape, jnp.float32),),
        in_specs=[vmem] * (2 * count + 1),
        out_specs=(vmem,) * (count + 1),
        scratch_shapes=[pltpu.VMEM((device_count,) + shape, jnp.bfloat16) for shape in shapes]
        + [pltpu.VMEM((chips,) + shape, jnp.bfloat16) for shape in shapes]
        + [pltpu.VMEM((chips - 1,) + shape, jnp.bfloat16) for shape in shapes]
        + [
            pltpu.VMEM(gains.shape, jnp.float32),
            pltpu.VMEM((chips,) + gains.shape, jnp.float32),
            pltpu.SemaphoreType.DMA((count, chips - 1)),
            pltpu.SemaphoreType.DMA((count, chips - 1)),
            pltpu.SemaphoreType.DMA((count, chips)),
            pltpu.SemaphoreType.DMA((count, chips)),
            pltpu.SemaphoreType.DMA((chips,)),
            pltpu.SemaphoreType.DMA((chips,)),
        ],
        compiler_params=pltpu.CompilerParams(
            collective_id=1, has_side_effects=True, vmem_limit_bytes=60 * 1024 * 1024
        ),
        cost_estimate=pl.CostEstimate(
            flops=flops, bytes_accessed=20 * sum(sizes) * device_count, transcendentals=0
        ),
        name="reduce_blocks",
    )(*lefts, *rights, gains)


def local_blocks(
    stream, segments, cotangent, attn_gain, mlp_gain, w_query, w_key, w_value, w_out, w_gate, w_up, w_down
):
    device_count = lax.axis_size("dp")
    rows = D // device_count
    tall_rows = FF // device_count
    padded = -(-rows // 16) * 16
    kv = KV * HD
    pad_rows = ((0, padded - rows), (0, 0))
    attn_rows = jnp.concatenate(
        [
            w_query.reshape(rows, D),
            w_key.reshape(rows, kv),
            w_value.reshape(rows, kv),
            w_out.reshape(rows, D),
        ],
        axis=1,
    )
    attn_all, gate_all, up_all, down_all = gather_blocks(
        (
            jnp.pad(attn_rows, pad_rows),
            jnp.pad(w_gate.reshape(rows, FF), pad_rows),
            jnp.pad(w_up.reshape(rows, FF), pad_rows),
            w_down.reshape(tall_rows, D),
        ),
        device_count,
    )
    spread = device_count * padded
    qkv_width = D + 2 * kv
    attn_all = attn_all.reshape(spread, qkv_width + D)
    qkv_weight = attn_all[:, :qkv_width]
    out_weight = attn_all[:, qkv_width:]
    gate_weight = gate_all.reshape(spread, FF)
    up_weight = up_all.reshape(spread, FF)
    down_weight = down_all.reshape(FF, D)

    source = lax.broadcasted_iota(jnp.int32, (D, spread), 0)
    target = lax.broadcasted_iota(jnp.int32, (D, spread), 1)
    placing = (source // rows) * padded + source % rows == target

    def place(value):
        return project(value, placing.astype(jnp.bfloat16)).astype(jnp.bfloat16)

    def unplace(value):
        return lax.dot_general(
            value,
            placing.astype(jnp.float32),
            (((1,), (1,)), ((), ())),
            precision=lax.Precision.HIGHEST,
            preferred_element_type=jnp.float32,
        )

    def unplace_b(value):
        return project_back(value, placing.astype(jnp.bfloat16)).astype(jnp.bfloat16)

    row_total = stream.shape[0]
    groups = row_total // MB_ROWS
    block_segments = segments.reshape(groups, MB_ROWS)
    cosine, sine_table = rotary_tables(block_segments)
    allowed = allowed_pairs(block_segments)
    root_attn = inverse_root(stream)
    normed_attn = place((stream * root_attn * attn_gain).astype(jnp.bfloat16))
    qkv = project(normed_attn, qkv_weight)
    query_proj = qkv[:, :D].reshape(groups, MB_ROWS, H, HD)
    key_proj = qkv[:, D : D + kv].reshape(groups, MB_ROWS, KV, HD)
    values = qkv[:, D + kv :].astype(jnp.bfloat16).reshape(groups, MB_ROWS, KV, HD)
    query_rot = (
        rotate(query_proj, cosine, sine_table)
        .astype(jnp.bfloat16)
        .reshape(groups, MB_ROWS, KV, GROUP, HD)
    )
    key_rot = rotate(key_proj, cosine, sine_table).astype(jnp.bfloat16)
    scores = attention_scores(query_rot, key_rot)
    exp_total = jnp.sum(jnp.where(allowed, jnp.exp(scores), 0.0), axis=-1, keepdims=True)
    log_total = jnp.log(exp_total)
    probs = jnp.where(allowed, jnp.exp(scores - log_total), 0.0)
    attn_probs = probs.astype(jnp.bfloat16)
    mixed_heads = place(
        batched("gkrij,gjkd->gikrd", attn_probs, values).astype(jnp.bfloat16).reshape(row_total, D)
    )
    hidden = stream + project(mixed_heads, out_weight)
    root_mlp = inverse_root(hidden)
    normed_mlp = place((hidden * root_mlp * mlp_gain).astype(jnp.bfloat16))
    gate_proj = project(normed_mlp, gate_weight)
    up_proj = project(normed_mlp, up_weight)
    sigmoid_gate = jax.nn.sigmoid(gate_proj)
    activation = (gate_proj * sigmoid_gate * up_proj).astype(jnp.bfloat16)
    output = hidden + project(activation, down_weight)

    live_rows = (segments >= 0).astype(jnp.float32)[:, None]
    grad_rows = cotangent * live_rows
    grad_rows_b = grad_rows.astype(jnp.bfloat16)
    grad_act = project_back(grad_rows_b, down_weight)
    grad_gate_b = (
        grad_act * up_proj * sigmoid_gate * (1.0 + gate_proj * (1.0 - sigmoid_gate))
    ).astype(jnp.bfloat16)
    grad_up_b = (grad_act * gate_proj * sigmoid_gate).astype(jnp.bfloat16)
    grad_normed_mlp = unplace(
        project_back(grad_gate_b, gate_weight) + project_back(grad_up_b, up_weight)
    )
    scaled_mlp = grad_normed_mlp * mlp_gain
    mlp_gain_term = jnp.sum(grad_normed_mlp * hidden * root_mlp, axis=0)
    grad_hidden = (
        grad_rows
        + root_mlp * scaled_mlp
        - hidden * root_mlp**3 * jnp.mean(scaled_mlp * hidden, axis=-1, keepdims=True)
    )
    grad_hidden_b = grad_hidden.astype(jnp.bfloat16)
    grad_mixed = unplace_b(
        project_back(grad_hidden_b, out_weight).astype(jnp.bfloat16)
    ).reshape(groups, MB_ROWS, KV, GROUP, HD)
    grad_probs = batched("gikrd,gjkd->gkrij", grad_mixed, values)
    inner_sum = jnp.sum(probs * grad_probs, axis=-1, keepdims=True)
    grad_scores = (probs * (grad_probs - inner_sum) * HD ** (-0.5)).astype(jnp.bfloat16)
    grad_q = batched("gkrij,gjkd->gikrd", grad_scores, key_rot).reshape(groups, MB_ROWS, H, HD)
    grad_k = batched("gkrij,gikrd->gjkd", grad_scores, query_rot)
    grad_v = batched("gkrij,gikrd->gjkd", attn_probs, grad_mixed)
    grad_qkv = jnp.concatenate(
        [
            unrotate(grad_q, cosine, sine_table).astype(jnp.bfloat16).reshape(row_total, D),
            unrotate(grad_k, cosine, sine_table).astype(jnp.bfloat16).reshape(row_total, kv),
            grad_v.astype(jnp.bfloat16).reshape(row_total, kv),
        ],
        axis=1,
    )
    grad_normed_attn = unplace(project_back(grad_qkv, qkv_weight))
    scaled_attn = grad_normed_attn * attn_gain
    attn_gain_term = jnp.sum(grad_normed_attn * stream * root_attn, axis=0)
    grad_x = (
        grad_hidden
        + root_attn * scaled_attn
        - stream * root_attn**3 * jnp.mean(scaled_attn * stream, axis=-1, keepdims=True)
    )
    gain_terms = jnp.stack([attn_gain_term, mlp_gain_term])
    attn_right = jnp.concatenate(
        [
            jnp.pad(grad_qkv, ((0, 0), (0, D))),
            jnp.pad(grad_hidden_b, ((0, 0), (qkv_width, 0))),
        ],
        axis=0,
    )
    attn_sum, gate_sum, up_sum, down_sum, gain_total = reduce_blocks(
        (
            jnp.concatenate([normed_attn, mixed_heads], axis=0).T,
            normed_mlp.T,
            normed_mlp.T,
            activation.T,
        ),
        (attn_right, grad_gate_b, grad_up_b, grad_rows_b),
        gain_terms,
        device_count,
    )
    grads = []
    begin = 0
    for width in (D, kv, kv, D):
        grads.append(attn_sum[:rows, begin : begin + width].reshape(-1))
        begin += width
    grads.append(gate_sum[:rows].reshape(-1))
    grads.append(up_sum[:rows].reshape(-1))
    grads.append(down_sum.reshape(-1))
    return (output, grad_x, *grads, gain_total[0], gain_total[1])


def solution(mesh):
    device_count = mesh.shape["dp"]
    aligned = D % device_count == 0 and FF % device_count == 0 and device_count % 8 == 0
    body = local_blocks if aligned and device_count >= 16 else local
    placed = (
        P("dp", None),
        P("dp"),
        P("dp", None),
        P(),
        P(),
        P("dp"),
        P("dp"),
        P("dp"),
        P("dp"),
        P("dp"),
        P("dp"),
        P("dp"),
    )
    return jax.shard_map(
        body,
        mesh=mesh,
        in_specs=placed,
        out_specs=(
            P("dp", None),
            P("dp", None),
            P("dp"),
            P("dp"),
            P("dp"),
            P("dp"),
            P("dp"),
            P("dp"),
            P("dp"),
            P(),
            P(),
        ),
        check_vma=False,
    )
```
